32 devices in a mesh: section: 4 (over y, x), tok: 4 (over z), mp: 2 (over core).
Axes of the slice: x: 2, y: 2, z: 4, core: 2. Of those that a mesh axis runs over, the one named last changes fastest.
Arguments:
- dense_in: bfloat16 [2, 256, 8192], P(None, 'tok', 'mp'), may hold values from -40 to 40
- pruned_gap: bfloat16 [2, 256, 8192], P(None, 'tok', 'mp'), may hold values from -3 to 3
- gain: float32 [4, 8192], P('section', 'mp'), may hold values from 0.5 to 1.5
- weights: bfloat16 [4, 512, 8192], P('section', 'tok', 'mp'), may hold values from -6 to 6
- mask_code: int32 [4, 512, 2048], P('section', None, 'mp'), may hold values from 0 to 5
- factor: float32 [4, 128, 128], P('section', 'mp'), may hold values from -1 to 2, as said below
Outputs:
- dense_window: bfloat16 [4, 2, 256, 512], P('section', None, 'tok', 'mp')
- pruned_window: bfloat16 [4, 2, 256, 512], P('section', None, 'tok', 'mp')
- gram: float32 [4, 128, 8192], P('section', 'tok', 'mp')
- cross: float32 [4, 128, 8192], P('section', 'tok', 'mp')
- corrected: float32 [4, 512, 128], P('section', None, 'mp')
The draws below stay inside these ranges and needn't reach their ends.
Inputs may be any that keep to these rules, and one draw needn't show every extreme that they name: `factor`: zero below the diagonal; diagonal entries between 0.5 and 2.
All inputs are finite; a program needn't handle non-finite values.
Results may differ from the reference program's by a relative error of at most 0.0079.
Values may be sent and summed in bfloat16 or wider, within the bound.
No kernel may reach another device: no remote copies, remote signals or barrier semaphores. Data moves between devices by JAX's collectives and lax.ppermute only.
A program may use at most 128 MiB of HBM per device.

```python
import math
import jax
import jax.numpy as jnp
from jax import lax

D = 8192
ROWS = 512
P_SIZE = 128
MICRO = 2
TOKENS = 256
SECTIONS = 4
STRIDE = 16
PANEL_STRIDE = 64


def draw_dense_in(key, part):
    key_rough, key_token, key_main = jax.random.split(key, 3)
    position = jnp.arange(D, dtype=jnp.float32) / D
    rough = jax.random.uniform(key_rough, (D,), jnp.float32, 0.5, 1.5)
    feature_scale = jnp.exp(math.log(3.0) * position) * rough
    token_scale = 0.5 * jnp.exp(jax.random.uniform(key_token, (MICRO, TOKENS, 1), jnp.float32, 0.0, math.log(10.0)))
    values_now = jax.random.normal(key_main, (MICRO, TOKENS, D), jnp.float32) * feature_scale * token_scale
    return jnp.clip(values_now, -40.0, 40.0).astype(jnp.bfloat16)


def draw_factor(key, part):
    key_diag, key_upper = jax.random.split(key, 2)
    diagonal_part = 0.5 * jnp.exp(jax.random.uniform(key_diag, (SECTIONS, P_SIZE), jnp.float32, 0.0, math.log(4.0)))
    upper_draw = jnp.clip(jax.random.normal(key_upper, (SECTIONS, P_SIZE, P_SIZE), jnp.float32) * 0.5, -1.0, 1.0)
    upper_part = jnp.triu(upper_draw, 1) / math.sqrt(P_SIZE)
    return upper_part + diagonal_part[:, :, None] * jnp.eye(P_SIZE, dtype=jnp.float32)[None]


def touch_ends(result, rng, smallest, largest):
    longest = result.shape.index(max(result.shape))
    spots = []
    for shift in (0, 1):
        where = [jax.random.randint(jax.random.fold_in(rng, axis), (), 0, length) for axis, length in enumerate(result.shape)]
        where[longest] = (where[longest] + shift) % result.shape[longest]
        spots.append(tuple(where))
    return result.at[spots[0]].set(smallest).at[spots[1]].set(largest)


def steps_of(key, shape, cuts, smallest, largest):
    def one(axis_at, blocks):
        steps = jax.random.uniform(jax.random.fold_in(jax.random.fold_in(key, 6), axis_at), (blocks,), jnp.float32, smallest / len(cuts), largest / len(cuts))
        return jnp.repeat(jnp.exp(steps), shape[axis_at] // blocks).reshape((-1,) + (1,) * (len(shape) - axis_at - 1))

    level = one(*cuts[0])
    for cut in cuts[1:]:
        level = level * one(*cut)
    return level


def normal_values(key, shape, deviation, most, shards=(), kind=jnp.bfloat16):
    result = jax.random.normal(key, shape, jnp.float32) * deviation
    if len(shards) > 0:
        result = steps_of(key, shape, shards, -0.22, 0.18) * result
    return jnp.clip(result, min=-most, max=most).astype(kind)


def setup_inputs(seed: int = 0) -> dict:
    streams_of = jax.random.split(jax.random.key(seed), 7)
    return {
        "dense_in": draw_dense_in(jax.random.fold_in(streams_of[6], 71), 0),
        "pruned_gap": normal_values(streams_of[1], (MICRO, TOKENS, D), 0.5, 3.0, ((1, 4), (2, 2))),
        "gain": jnp.clip(1.0 + 0.1 * jax.random.normal(streams_of[2], (SECTIONS, D), jnp.float32), 0.5, 1.5),
        "weights": normal_values(streams_of[3], (SECTIONS, ROWS, D), 1.0, 6.0, ((0, 4), (1, 4), (2, 2))),
        "mask_code": touch_ends(jax.random.randint(streams_of[4], (SECTIONS, ROWS, D // 4), 0, 6), jax.random.fold_in(streams_of[4], 1), 0, 5).astype(jnp.int32),
        "factor": draw_factor(jax.random.fold_in(streams_of[6], 71), 0),
    }


def expand_keep(mask_codes):
    first_pos = mask_codes < 3
    second_pos = (mask_codes == 0) | (mask_codes == 3) | (mask_codes == 4)
    third_pos = (mask_codes == 1) | (mask_codes == 3) | (mask_codes == 5)
    fourth_pos = (mask_codes == 2) | (mask_codes == 4) | (mask_codes == 5)
    spread = jnp.stack([first_pos, second_pos, third_pos, fourth_pos], axis=-1)
    return spread.reshape(mask_codes.shape[0], mask_codes.shape[1] * 4)

def normalize(states, gain_row):
    widened = states.astype(jnp.float32)
    mean_square = lax.optimization_barrier(jnp.mean(widened * widened, axis=-1, keepdims=True))
    return (widened * lax.rsqrt(mean_square + 1e-06) * gain_row).astype(jnp.bfloat16)

def window_of(states, column_total, stride_len):
    return states.reshape(states.shape[0], column_total, stride_len)[:, :, 0]

def with_window(states, window, stride_len):
    shaped = states.reshape(states.shape[0], window.shape[1], stride_len)
    joined = jnp.concatenate([window[:, :, None], shaped[:, :, 1:]], axis=2)
    return joined.reshape(states.shape)

def reference(dense_in, pruned_gap, gain, weights, mask_code, factor):
    token_total = MICRO * TOKENS
    inv_root = 1.0 / math.sqrt(D)
    highest = lax.Precision.HIGHEST
    dense_flat = dense_in.reshape(token_total, D)
    pruned_flat = (dense_in.astype(jnp.float32) + pruned_gap.astype(jnp.float32)).astype(jnp.bfloat16).reshape(token_total, D)
    dense_windows = []
    pruned_windows = []
    gram_list = []
    cross_list = []
    corrections = []
    for section_num in range(SECTIONS):
        keep_mask = expand_keep(mask_code[section_num])
        weight_now = weights[section_num]
        weight_pruned = jnp.where(keep_mask, weight_now, jnp.zeros_like(weight_now))
        normed_dense = normalize(dense_flat, gain[section_num])
        normed_pruned = normalize(pruned_flat, gain[section_num])
        out_dense = jnp.dot(normed_dense, weight_now.T, preferred_element_type=jnp.float32) * inv_root
        out_pruned = jnp.dot(normed_pruned, weight_pruned.T, preferred_element_type=jnp.float32) * inv_root
        window_dense = (window_of(dense_flat, ROWS, STRIDE).astype(jnp.float32) + out_dense).astype(jnp.bfloat16)
        window_pruned = (window_of(pruned_flat, ROWS, STRIDE).astype(jnp.float32) + out_pruned).astype(jnp.bfloat16)
        dense_flat = with_window(dense_flat, window_dense, STRIDE)
        pruned_flat = with_window(pruned_flat, window_pruned, STRIDE)
        dense_windows.append(window_dense.reshape(MICRO, TOKENS, ROWS))
        pruned_windows.append(window_pruned.reshape(MICRO, TOKENS, ROWS))
        panel_cols = window_of(normed_pruned, P_SIZE, PANEL_STRIDE)
        gram_now = jnp.dot(panel_cols.T, normed_pruned, preferred_element_type=jnp.float32) / token_total
        cross_now = jnp.dot(panel_cols.T, normed_dense, preferred_element_type=jnp.float32) / token_total
        residual = jnp.dot(weight_now.astype(jnp.float32), cross_now.T, precision=highest) - jnp.dot(weight_pruned.astype(jnp.float32), gram_now.T, precision=highest)
        factor_now = factor[section_num]
        inner_left = jnp.dot(residual, factor_now.T, precision=highest)
        correction = jnp.dot(inner_left, factor_now, precision=highest)
        keep_panel = window_of(keep_mask, P_SIZE, PANEL_STRIDE).astype(jnp.float32)
        weight_panel = window_of(weight_now, P_SIZE, PANEL_STRIDE).astype(jnp.float32)
        gram_list.append(gram_now)
        cross_list.append(cross_now)
        corrections.append(keep_panel * (weight_panel + correction))
    return (jnp.stack(dense_windows), jnp.stack(pruned_windows), jnp.stack(gram_list), jnp.stack(cross_list), jnp.stack(corrections))
```

```python
import math

import jax
import jax.numpy as jnp
from jax import lax
from jax.sharding import PartitionSpec as P


STREAMS = 2


def partner(block, axis, distance):
    route = [(i, i ^ distance) for i in range(lax.axis_size(axis))]
    return lax.ppermute(block, axis, route)


def pick(array, index, axis=0):
    return lax.dynamic_index_in_dim(array, index, axis, keepdims=False)


def placed(pieces, me, axis, size):
    shape = list(pieces[0].shape)
    shape[axis] = size * len(pieces)
    whole = jnp.zeros(shape, pieces[0].dtype)
    for d, piece in enumerate(pieces):
        whole = lax.dynamic_update_slice_in_dim(whole, piece, (me ^ d) * size, axis)
    return whole


def tree_sum(pieces):
    while len(pieces) > 1:
        pieces = [a + b for a, b in zip(pieces[0::2], pieces[1::2])]
    return pieces[0]


def exchange(chunks, axis):
    me = lax.axis_index(axis)
    out = [pick(chunks, me)]
    for d in range(1, lax.axis_size(axis)):
        out.append(partner(pick(chunks, me ^ d), axis, d))
    return out


def gather(block, axis):
    return [block] + [partner(block, axis, d) for d in range(1, lax.axis_size(axis))]


def keep_of(codes, position):
    first = codes < 3
    second = (codes == 0) | (codes == 3) | (codes == 4)
    third = (codes == 1) | (codes == 3) | (codes == 5)
    fourth = (codes == 2) | (codes == 4) | (codes == 5)
    return jnp.where(
        position == 0, first, jnp.where(position == 1, second, jnp.where(position == 2, third, fourth))
    )


def spread_matrix(count, stride, dtype=jnp.bfloat16):
    rows = lax.broadcasted_iota(jnp.int32, (count, count * stride), 0)
    cols = lax.broadcasted_iota(jnp.int32, (count, count * stride), 1)
    return rows, cols


def dot_t(a, b):
    return lax.dot_general(a, b, (((1,), (1,)), ((), ())), preferred_element_type=jnp.float32)


def on_device(dense_in, pruned_gap, gain, weights, mask_code, factor):
    bf16, f32 = jnp.bfloat16, jnp.float32
    highest = lax.Precision.HIGHEST
    n_sec, n_tok, n_mp = (lax.axis_size(a) for a in ("section", "tok", "mp"))
    sec, tok, mp = (lax.axis_index(a) for a in ("section", "tok", "mp"))
    micro, tok_rows, width_local = dense_in.shape
    tokens = micro * tok_rows
    rows_local = weights.shape[1]
    rows = rows_local * n_tok
    width = width_local * n_mp
    stride = width // rows
    panel_local = factor.shape[1]
    panel = panel_local * n_mp
    panel_step = rows // panel
    token_total = tokens * n_tok
    win_local = width_local // stride
    quarter = width_local // n_tok
    sub = quarter // n_sec
    win_quarter = quarter // stride
    blocks = n_mp // STREAMS
    tok_sub = tokens // blocks
    inv_root = 1.0 / math.sqrt(width)

    gain_row = gain[0]
    own_weights = weights[0]
    codes = mask_code[0]
    dense = dense_in.reshape(tokens, width_local)
    gap = pruned_gap.reshape(tokens, width_local)
    pruned = (dense.astype(f32) + gap.astype(f32)).astype(bf16)
    both = jnp.stack([dense, pruned])

    split = both.reshape(STREAMS, tokens, n_tok, n_sec, sub)
    own_sub = pick(split, sec, 3)
    x_blocks = [pick(both.reshape(STREAMS, tokens, n_tok, quarter), tok, 2)]
    landed = [partner(pick(own_sub, tok ^ d, 2), "tok", d) for d in range(1, n_tok)]
    for block in landed:
        x_blocks.append(placed(gather(block, "section"), sec, 2, sub))

    w_split = own_weights.reshape(rows_local, n_tok, quarter)
    w_pieces = [pick(w_split, tok, 1)]
    w_pieces += [partner(pick(w_split, tok ^ d, 1), "tok", d) for d in range(1, n_tok)]
    w_quarter = placed(w_pieces, tok, 0, rows_local)
    own_win = own_weights.reshape(rows_local, win_local, stride)[:, :, 0]
    win_half = placed(gather(own_win, "tok"), tok, 0, rows_local)
    keep_win = codes.reshape(rows, win_local, stride // 4)[:, :, 0] < 3
    win_kept = jnp.where(keep_win, win_half, jnp.zeros_like(win_half))
    by_stream = jnp.stack([win_half, win_kept])
    win_stream = placed(
        exchange(jnp.tile(by_stream, (blocks, 1, 1)), "mp"), mp, 1, win_local
    )

    def to_carriers(array):
        shaped = array.reshape(STREAMS, blocks, tok_sub, *array.shape[2:])
        return jnp.moveaxis(shaped, 1, 0).reshape(n_mp, tok_sub, *array.shape[2:])

    base_win = both.reshape(STREAMS, tokens, win_local, stride)[:, :, :, 0]
    window = placed(exchange(to_carriers(base_win), "mp"), mp, 1, win_local)
    feature = lax.broadcasted_iota(jnp.int32, (1, 1, width_local), 2)
    wide = jnp.where(feature % stride == 0, 0.0, both.astype(f32))
    squares = jnp.sum(wide * wide, axis=2)
    base_square = tree_sum(exchange(to_carriers(squares), "mp"))
    gain_win = placed(
        gather(gain_row.reshape(win_local, stride)[:, 0], "mp"), mp, 0, win_local
    )
    whole_factor = placed(gather(factor[0], "mp"), mp, 0, panel_local)

    codes_q = lax.dynamic_slice_in_dim(codes, tok * (quarter // 4), quarter // 4, 1)
    group_row = lax.broadcasted_iota(jnp.int32, (quarter // 4, quarter), 0)
    group_col = lax.broadcasted_iota(jnp.int32, (quarter // 4, quarter), 1)
    spread4 = (group_col // 4 == group_row).astype(bf16)
    codes_f = jnp.dot(codes_q.astype(bf16), spread4, preferred_element_type=f32)
    lane = lax.broadcasted_iota(jnp.int32, (1, quarter), 1)
    keep_q = keep_of(codes_f, lane % 4)
    gain_q = lax.dynamic_slice_in_dim(gain_row, tok * quarter, quarter, 0)[None]
    fixed_gain = jnp.where(lane % stride == 0, 0.0, gain_q)
    dense_gw = (w_quarter.astype(f32) * fixed_gain).astype(bf16)
    pruned_gw = jnp.where(keep_q, dense_gw, jnp.zeros_like(dense_gw))
    x_all = jnp.stack(x_blocks)
    part = jnp.stack(
        [
            dot_t(x_all[:, 0].reshape(token_total, quarter), dense_gw),
            dot_t(x_all[:, 1].reshape(token_total, quarter), pruned_gw),
        ]
    ).astype(bf16)
    part = part.reshape(STREAMS, n_tok, blocks, tok_sub, rows)
    part = part.transpose(2, 0, 1, 3, 4).reshape(n_mp, n_tok, tok_sub, rows)
    part = tree_sum([p.astype(f32) for p in exchange(part, "mp")]).astype(bf16)
    landed = [part[0]] + [partner(part[d], "tok", d) for d in range(1, n_tok)]
    fixed_part = tree_sum([p.astype(f32) for p in landed])

    def layer(now):
        wide_now = now.astype(f32)
        square = base_square + jnp.sum(wide_now * wide_now, axis=1)
        scale = lax.rsqrt(square / width + 1e-06)[:, None]
        normed_now = (wide_now * scale * gain_win).astype(bf16)
        out = (fixed_part * scale + dot_t(normed_now, win_stream)) * inv_root
        return (wide_now + out).astype(bf16), normed_now, scale

    for step in range(n_sec - 1):
        after, _, _ = layer(window)
        arrived = lax.ppermute(after, "section", [(step, step + 1)])
        window = jnp.where(sec == step + 1, arrived, window)
    after, normed_win, scale = layer(window)

    def from_carriers(pieces):
        stacked = placed([p[None] for p in pieces], mp, 0, 1)
        shaped = stacked.reshape(blocks, STREAMS, tok_sub, *pieces[0].shape[1:])
        return jnp.moveaxis(shaped, 1, 0).reshape(STREAMS, tokens, *pieces[0].shape[1:])

    def features_out(array):
        return jnp.moveaxis(array.reshape(tok_sub, n_mp, win_local), 1, 0)

    windows = from_carriers(exchange(features_out(after), "mp"))
    normed_half = from_carriers(exchange(features_out(normed_win), "mp"))
    own_panel = normed_win.reshape(tok_sub, panel, panel_step)[:, :, 0]
    panel_cols = from_carriers(gather(own_panel, "mp"))[1]
    scales = from_carriers(gather(scale[:, 0], "mp"))

    to_tok = normed_half.reshape(STREAMS, tokens, n_tok, win_quarter)
    panel_all = gather(panel_cols, "tok")
    scales_all = gather(scales, "tok")
    normed_all = exchange(jnp.moveaxis(to_tok, 2, 0), "tok")
    panel_rows = jnp.concatenate(panel_all, axis=0)
    win_row = lax.broadcasted_iota(jnp.int32, (win_quarter, quarter), 0)
    win_col = lax.broadcasted_iota(jnp.int32, (win_quarter, quarter), 1)
    spread_win = (win_col == win_row * stride).astype(bf16)
    grams = []
    for stream in range(STREAMS):
        x_stream = x_all[:, stream].reshape(token_total, quarter)
        factor_t = jnp.concatenate([s[stream] for s in scales_all])[:, None]
        win_n = jnp.concatenate([n[stream] for n in normed_all], axis=0)
        filled = jnp.dot(win_n, spread_win, preferred_element_type=f32)
        normed = jnp.where(lane % stride == 0, filled, x_stream.astype(f32) * factor_t * gain_q)
        grams.append(
            lax.dot_general(
                panel_rows,
                normed.astype(bf16),
                (((0,), (0,)), ((), ())),
                preferred_element_type=f32,
            )
            / token_total
        )
    high = [g.astype(bf16) for g in grams]
    low = [(g - h.astype(f32)).astype(bf16) for g, h in zip(grams, high)]
    kept_q = jnp.where(keep_q, w_quarter, jnp.zeros_like(w_quarter))
    residual = (dot_t(w_quarter, high[0]) - dot_t(kept_q, high[1])) + (
        dot_t(w_quarter, low[0]) - dot_t(kept_q, low[1])
    )
    squared = lax.dot_general(
        whole_factor, whole_factor, (((0,), (0,)), ((), ())), precision=highest
    )
    correction = jnp.dot(residual, squared, precision=highest)
    column_chunks = jnp.moveaxis(correction.reshape(rows, n_mp, panel_local), 1, 0)
    correction = tree_sum(exchange(column_chunks, "mp")).astype(bf16)
    correction = tree_sum([c.astype(f32) for c in gather(correction, "tok")])
    keep_panel = keep_win.reshape(rows, panel_local, panel_step)[:, :, 0]
    weight_panel = win_half.reshape(rows, panel_local, panel_step)[:, :, 0].astype(f32)
    corrected = jnp.where(keep_panel, weight_panel + correction, 0.0)

    out_grams = []
    for g in (high[1], high[0]):
        pieces = exchange(g.reshape(n_tok, panel // n_tok, quarter), "tok")
        out_grams.append(placed(pieces, tok, 1, quarter).astype(f32)[None])
    windows = windows.reshape(STREAMS, micro, tok_rows, win_local)
    return windows[0][None], windows[1][None], out_grams[0], out_grams[1], corrected[None]


def solution(mesh):
    in_specs = (
        P(None, "tok", "mp"),
        P(None, "tok", "mp"),
        P("section", "mp"),
        P("section", "tok", "mp"),
        P("section", None, "mp"),
        P("section", "mp", None),
    )
    out_specs = (
        P("section", None, "tok", "mp"),
        P("section", None, "tok", "mp"),
        P("section", "tok", "mp"),
        P("section", "tok", "mp"),
        P("section", None, "mp"),
    )
    return jax.shard_map(
        on_device, mesh=mesh, in_specs=in_specs, out_specs=out_specs, check_vma=False
    )
```

```python
import math

import jax
import jax.numpy as jnp
from jax import lax
from jax.experimental import pallas as pl
from jax.experimental.pallas import tpu as pltpu
from jax.sharding import PartitionSpec as P


STREAMS = 2


def partner(block, axis, distance):
    route = [(i, i ^ distance) for i in range(lax.axis_size(axis))]
    return lax.ppermute(block, axis, route)


def pick(array, index, axis=0):
    return lax.dynamic_index_in_dim(array, index, axis, keepdims=False)


def placed(pieces, me, axis, size):
    shape = list(pieces[0].shape)
    shape[axis] = size * len(pieces)
    whole = jnp.zeros(shape, pieces[0].dtype)
    for d, piece in enumerate(pieces):
        whole = lax.dynamic_update_slice_in_dim(whole, piece, (me ^ d) * size, axis)
    return whole


def tree_sum(pieces):
    while len(pieces) > 1:
        pieces = [a + b for a, b in zip(pieces[0::2], pieces[1::2])]
    return pieces[0]


def exchange(chunks, axis):
    me = lax.axis_index(axis)
    out = [pick(chunks, me)]
    for d in range(1, lax.axis_size(axis)):
        out.append(partner(pick(chunks, me ^ d), axis, d))
    return out


def gather(block, axis):
    return [block] + [partner(block, axis, d) for d in range(1, lax.axis_size(axis))]


def keep_of(codes, position):
    first = codes < 3
    second = (codes == 0) | (codes == 3) | (codes == 4)
    third = (codes == 1) | (codes == 3) | (codes == 5)
    fourth = (codes == 2) | (codes == 4) | (codes == 5)
    return jnp.where(
        position == 0, first, jnp.where(position == 1, second, jnp.where(position == 2, third, fourth))
    )


def spread_matrix(count, stride, dtype=jnp.bfloat16):
    rows = lax.broadcasted_iota(jnp.int32, (count, count * stride), 0)
    cols = lax.broadcasted_iota(jnp.int32, (count, count * stride), 1)
    return rows, cols


def dot_t(a, b):
    return lax.dot_general(a, b, (((1,), (1,)), ((), ())), preferred_element_type=jnp.float32)


def on_device(dense_in, pruned_gap, gain, weights, mask_code, factor):
    bf16, f32 = jnp.bfloat16, jnp.float32
    highest = lax.Precision.HIGHEST
    n_sec, n_tok, n_mp = (lax.axis_size(a) for a in ("section", "tok", "mp"))
    sec, tok, mp = (lax.axis_index(a) for a in ("section", "tok", "mp"))
    micro, tok_rows, width_local = dense_in.shape
    tokens = micro * tok_rows
    rows_local = weights.shape[1]
    rows = rows_local * n_tok
    width = width_local * n_mp
    stride = width // rows
    panel_local = factor.shape[1]
    panel = panel_local * n_mp
    panel_step = rows // panel
    token_total = tokens * n_tok
    win_local = width_local // stride
    quarter = width_local // n_tok
    sub = quarter // n_sec
    win_quarter = quarter // stride
    blocks = n_mp // STREAMS
    tok_sub = tokens // blocks
    inv_root = 1.0 / math.sqrt(width)

    gain_row = gain[0]
    own_weights = weights[0]
    codes = mask_code[0]
    dense = dense_in.reshape(tokens, width_local)
    gap = pruned_gap.reshape(tokens, width_local)
    pruned = (dense.astype(f32) + gap.astype(f32)).astype(bf16)
    both = jnp.stack([dense, pruned])

    split = both.reshape(STREAMS, tokens, n_tok, n_sec, sub)
    own_sub = pick(split, sec, 3)
    x_blocks = [pick(both.reshape(STREAMS, tokens, n_tok, quarter), tok, 2)]
    landed = [partner(pick(own_sub, tok ^ d, 2), "tok", d) for d in range(1, n_tok)]
    for block in landed:
        x_blocks.append(placed(gather(block, "section"), sec, 2, sub))

    w_split = own_weights.reshape(rows_local, n_tok, quarter)
    w_pieces = [pick(w_split, tok, 1)]
    w_pieces += [partner(pick(w_split, tok ^ d, 1), "tok", d) for d in range(1, n_tok)]
    w_quarter = placed(w_pieces, tok, 0, rows_local)
    own_win = own_weights.reshape(rows_local, win_local, stride)[:, :, 0]
    win_half = placed(gather(own_win, "tok"), tok, 0, rows_local)
    keep_win = codes.reshape(rows, win_local, stride // 4)[:, :, 0] < 3
    win_kept = jnp.where(keep_win, win_half, jnp.zeros_like(win_half))
    by_stream = jnp.stack([win_half, win_kept])
    win_stream = placed(
        exchange(jnp.tile(by_stream, (blocks, 1, 1)), "mp"), mp, 1, win_local
    )

    def to_carriers(array):
        shaped = array.reshape(STREAMS, blocks, tok_sub, *array.shape[2:])
        return jnp.moveaxis(shaped, 1, 0).reshape(n_mp, tok_sub, *array.shape[2:])

    base_win = both.reshape(STREAMS, tokens, win_local, stride)[:, :, :, 0]
    window = placed(exchange(to_carriers(base_win), "mp"), mp, 1, win_local)
    feature = lax.broadcasted_iota(jnp.int32, (1, 1, width_local), 2)
    wide = jnp.where(feature % stride == 0, 0.0, both.astype(f32))
    squares = jnp.sum(wide * wide, axis=2)
    base_square = tree_sum(exchange(to_carriers(squares), "mp"))
    gain_win = placed(
        gather(gain_row.reshape(win_local, stride)[:, 0], "mp"), mp, 0, win_local
    )
    whole_factor = placed(gather(factor[0], "mp"), mp, 0, panel_local)

    codes_q = lax.dynamic_slice_in_dim(codes, tok * (quarter // 4), quarter // 4, 1)
    group_row = lax.broadcasted_iota(jnp.int32, (quarter // 4, quarter), 0)
    group_col = lax.broadcasted_iota(jnp.int32, (quarter // 4, quarter), 1)
    spread4 = (group_col // 4 == group_row).astype(bf16)
    codes_f = jnp.dot(codes_q.astype(bf16), spread4, preferred_element_type=f32)
    lane = lax.broadcasted_iota(jnp.int32, (1, quarter), 1)
    keep_q = keep_of(codes_f, lane % 4)
    gain_q = lax.dynamic_slice_in_dim(gain_row, tok * quarter, quarter, 0)[None]
    fixed_gain = jnp.where(lane % stride == 0, 0.0, gain_q)
    dense_gw = (w_quarter.astype(f32) * fixed_gain).astype(bf16)
    pruned_gw = jnp.where(keep_q, dense_gw, jnp.zeros_like(dense_gw))
    x_all = jnp.stack(x_blocks)
    part = jnp.stack(
        [
            dot_t(x_all[:, 0].reshape(token_total, quarter), dense_gw),
            dot_t(x_all[:, 1].reshape(token_total, quarter), pruned_gw),
        ]
    ).astype(bf16)
    part = part.reshape(STREAMS, n_tok, blocks, tok_sub, rows)
    part = part.transpose(2, 0, 1, 3, 4).reshape(n_mp, n_tok, tok_sub, rows)
    part = tree_sum([p.astype(f32) for p in exchange(part, "mp")]).astype(bf16)
    landed = [part[0]] + [partner(part[d], "tok", d) for d in range(1, n_tok)]
    fixed_part = tree_sum([p.astype(f32) for p in landed])

    def layer(now):
        wide_now = now.astype(f32)
        square = base_square + jnp.sum(wide_now * wide_now, axis=1)
        scale = lax.rsqrt(square / width + 1e-06)[:, None]
        normed_now = (wide_now * scale * gain_win).astype(bf16)
        out = (fixed_part * scale + dot_t(normed_now, win_stream)) * inv_root
        return (wide_now + out).astype(bf16), normed_now, scale

    for step in range(n_sec - 1):
        after, _, _ = layer(window)
        arrived = lax.ppermute(after, "section", [(step, step + 1)])
        window = jnp.where(sec == step + 1, arrived, window)
    after, normed_win, scale = layer(window)

    def from_carriers(pieces):
        stacked = placed([p[None] for p in pieces], mp, 0, 1)
        shaped = stacked.reshape(blocks, STREAMS, tok_sub, *pieces[0].shape[1:])
        return jnp.moveaxis(shaped, 1, 0).reshape(STREAMS, tokens, *pieces[0].shape[1:])

    def features_out(array):
        return jnp.moveaxis(array.reshape(tok_sub, n_mp, win_local), 1, 0)

    windows = from_carriers(exchange(features_out(after), "mp"))
    normed_half = from_carriers(exchange(features_out(normed_win), "mp"))
    own_panel = normed_win.reshape(tok_sub, panel, panel_step)[:, :, 0]
    panel_cols = from_carriers(gather(own_panel, "mp"))[1]
    scales = from_carriers(gather(scale[:, 0], "mp"))

    to_tok = normed_half.reshape(STREAMS, tokens, n_tok, win_quarter)
    panel_all = gather(panel_cols, "tok")
    scales_all = gather(scales, "tok")
    normed_all = exchange(jnp.moveaxis(to_tok, 2, 0), "tok")
    panel_rows = jnp.concatenate(panel_all, axis=0)
    win_row = lax.broadcasted_iota(jnp.int32, (win_quarter, quarter), 0)
    win_col = lax.broadcasted_iota(jnp.int32, (win_quarter, quarter), 1)
    spread_win = (win_col == win_row * stride).astype(bf16)
    grams = []
    for stream in range(STREAMS):
        x_stream = x_all[:, stream].reshape(token_total, quarter)
        factor_t = jnp.concatenate([s[stream] for s in scales_all])[:, None]
        win_n = jnp.concatenate([n[stream] for n in normed_all], axis=0)
        filled = jnp.dot(win_n, spread_win, preferred_element_type=f32)
        normed = jnp.where(lane % stride == 0, filled, x_stream.astype(f32) * factor_t * gain_q)
        grams.append(
            lax.dot_general(
                panel_rows,
                normed.astype(bf16),
                (((0,), (0,)), ((), ())),
                preferred_element_type=f32,
            )
            / token_total
        )
    high = [g.astype(bf16) for g in grams]
    low = [(g - h.astype(f32)).astype(bf16) for g, h in zip(grams, high)]
    kept_q = jnp.where(keep_q, w_quarter, jnp.zeros_like(w_quarter))
    residual = (dot_t(w_quarter, high[0]) - dot_t(kept_q, high[1])) + (
        dot_t(w_quarter, low[0]) - dot_t(kept_q, low[1])
    )
    squared = lax.dot_general(
        whole_factor, whole_factor, (((0,), (0,)), ((), ())), precision=highest
    )
    correction = jnp.dot(residual, squared, precision=highest)
    column_chunks = jnp.moveaxis(correction.reshape(rows, n_mp, panel_local), 1, 0)
    correction = tree_sum(exchange(column_chunks, "mp")).astype(bf16)
    correction = tree_sum([c.astype(f32) for c in gather(correction, "tok")])
    keep_panel = keep_win.reshape(rows, panel_local, panel_step)[:, :, 0]
    weight_panel = win_half.reshape(rows, panel_local, panel_step)[:, :, 0].astype(f32)
    corrected = jnp.where(keep_panel, weight_panel + correction, 0.0)

    out_grams = []
    for g in (high[1], high[0]):
        pieces = exchange(g.reshape(n_tok, panel // n_tok, quarter), "tok")
        out_grams.append(placed(pieces, tok, 1, quarter).astype(f32)[None])
    windows = windows.reshape(STREAMS, micro, tok_rows, win_local)
    return windows[0][None], windows[1][None], out_grams[0], out_grams[1], corrected[None]


def run(name, body, outs, *args, scratch=()):
    vmem = pl.BlockSpec(memory_space=pltpu.VMEM)
    return pl.pallas_call(
        body,
        out_shape=outs,
        in_specs=[vmem] * len(args),
        out_specs=jax.tree.map(lambda _: vmem, outs),
        scratch_shapes=scratch,
        name=name,
    )(*args)


def shape_of(dims, dtype):
    return jax.ShapeDtypeStruct(dims, dtype)


def aligned(index, size):
    return pl.ds(pl.multiple_of(index * size, size), size)


def iota2(shape, axis):
    return lax.broadcasted_iota(jnp.int32, shape, axis)


def one_hot(shape, wanted_row):
    return jnp.where(iota2(shape, 0) == wanted_row(iota2(shape, 1)), 1.0, 0.0).astype(jnp.bfloat16)


def mm(a, b, dims=((1,), (0,)), **kw):
    return lax.dot_general(a, b, (dims, ((), ())), preferred_element_type=jnp.float32, **kw)


def fast_on_device(dense_in, pruned_gap, gain, weights, mask_code, factor):
    bf16, f32 = jnp.bfloat16, jnp.float32
    highest = lax.Precision.HIGHEST
    n_sec, n_tok, n_mp = (lax.axis_size(a) for a in ("section", "tok", "mp"))
    micro, tok_rows, width_local = dense_in.shape
    tokens = micro * tok_rows
    rows_local = weights.shape[1]
    rows = rows_local * n_tok
    width = width_local * n_mp
    stride = width // rows
    panel_local = factor.shape[1]
    panel = panel_local * n_mp
    panel_step = rows // panel
    panel_own = panel // n_tok
    token_total = tokens * n_tok
    win_local = width_local // stride
    quarter = width_local // n_tok
    sub = quarter // n_sec
    win_quarter = quarter // stride
    inv_root = 1.0 / math.sqrt(width)
    lanes = 128
    chunk = lanes * stride
    sec, tok, mp = (lax.axis_index(a) for a in ("section", "tok", "mp"))

    def load_pair(d_ref, g_ref, span):
        dense = jnp.concatenate([d_ref[i, :, span] for i in range(micro)], axis=0)
        gap = jnp.concatenate([g_ref[i, :, span] for i in range(micro)], axis=0)
        return dense, (dense.astype(f32) + gap.astype(f32)).astype(bf16)

    def x_send(d_ref, g_ref, *outs):
        s, t = lax.axis_index("section"), lax.axis_index("tok")
        for d in range(1, n_tok):
            pair = load_pair(d_ref, g_ref, aligned((t ^ d) * n_sec + s, sub))
            outs[d - 1][0], outs[d - 1][1] = pair

    pieces = run(
        "x_send", x_send, [shape_of((2, tokens, sub), bf16)] * (n_tok - 1), dense_in, pruned_gap
    )
    landed = [partner(p, "tok", d + 1) for d, p in enumerate(pieces)]
    x_parts = [gather(p, "section") for p in landed]

    def select_windows(load, store):
        pattern = one_hot((chunk, lanes), lambda c: c * stride)
        for i in range(width_local // chunk):
            store(slice(i * lanes, (i + 1) * lanes), mm(load(slice(i * chunk, (i + 1) * chunk)), pattern))

    def w_send(w_ref, win_ref, own_ref, *outs):
        t = lax.axis_index("tok")
        own_ref[...] = w_ref[0, :, aligned(t, quarter)]
        for d in range(1, n_tok):
            outs[d - 1][...] = w_ref[0, :, aligned(t ^ d, quarter)]

        def store(span, value):
            win_ref[:, span] = value.astype(bf16)

        select_windows(lambda span: w_ref[0, :, span], store)

    w_out = run(
        "w_send",
        w_send,
        [shape_of((rows_local, win_local), bf16)] + [shape_of((rows_local, quarter), bf16)] * n_tok,
        weights,
    )
    w_pieces = [w_out[1]] + [partner(p, "tok", d + 1) for d, p in enumerate(w_out[2:])]
    win_pieces = gather(w_out[0], "tok")

    def x_keep(d_ref, g_ref, own_ref, win_keep, win_send, sq_keep, sq_send, both):
        t, m = lax.axis_index("tok"), lax.axis_index("mp")
        both[0], both[1] = load_pair(d_ref, g_ref, slice(None))
        own_ref[...] = both[:, :, aligned(t, quarter)]
        fixed = iota2((1, width_local), 1) % stride != 0
        for which, win_ref, sq_ref in ((m, win_keep, sq_keep), (1 - m, win_send, sq_send)):

            def store(span, value, win_ref=win_ref):
                win_ref[:, span] = value.astype(bf16)

            select_windows(lambda span, which=which: both[which, :, span], store)
            value = both[which].astype(f32)
            total = jnp.sum(jnp.where(fixed, value * value, 0.0), axis=1, keepdims=True)
            sq_ref[...] = jnp.broadcast_to(total, sq_ref.shape)

    x_own, bw_keep, bw_send, sq_keep, sq_send = run(
        "x_keep",
        x_keep,
        [
            shape_of((2, tokens, quarter), bf16),
            shape_of((tokens, win_local), bf16),
            shape_of((tokens, win_local), bf16),
            shape_of((tokens, lanes), f32),
            shape_of((tokens, lanes), f32),
        ],
        dense_in,
        pruned_gap,
        scratch=[pltpu.VMEM((2, tokens, width_local), bf16)],
    )
    bw_other = partner(bw_send, "mp", 1)
    sq_other = partner(sq_send, "mp", 1)

    def masks(c_ref, keep_ref, keep_win_ref):
        t = lax.axis_index("tok")
        groups = quarter // 4
        codes = c_ref[0, :, aligned(t, groups)].astype(f32).astype(bf16)
        at = jnp.where(
            iota2((groups, quarter), 0) == iota2((groups, quarter), 1) // 4, 1.0, 0.0
        ).astype(bf16)
        spread = mm(codes, at)
        position = iota2((1, quarter), 1) % 4
        keep = jnp.zeros(spread.shape, f32)
        for code, kept in enumerate(((0, 1), (0, 2), (0, 3), (1, 2), (1, 3), (2, 3))):
            here = jnp.where((position == kept[0]) | (position == kept[1]), 1.0, 0.0)
            keep = jnp.where(spread == code, here, keep)
        keep_ref[...] = keep.astype(bf16)
        all_codes = c_ref[0].astype(f32).astype(bf16)
        pattern = one_hot((width_local // 4, win_local), lambda c: c * (stride // 4))
        keep_win_ref[...] = jnp.where(mm(all_codes, pattern) < 2.5, 1.0, 0.0).astype(bf16)

    keep_q, keep_win = run(
        "masks", masks, [shape_of((rows, quarter), bf16), shape_of((rows, win_local), bf16)], mask_code
    )

    def win_weights(k_ref, *refs):
        ins, (keep_ref, send_ref, panel_ref, whole) = refs[:n_tok], refs[n_tok:]
        t, m = lax.axis_index("tok"), lax.axis_index("mp")
        for d in range(n_tok):
            whole[aligned(t ^ d, rows_local), :] = ins[d][...]
        dense = whole[...]
        kept = dense * k_ref[...]
        turned = jnp.concatenate([kept[rows // 2 :], kept[: rows // 2]], axis=0)
        keep_ref[...] = jnp.where(m == 0, dense, turned)
        send_ref[...] = jnp.where(m == 0, turned, dense)
        pattern = one_hot((win_local, panel_local), lambda c: c * panel_step)
        panel_ref[:, :panel_local] = mm(kept, pattern)
        panel_ref[:, panel_local:] = mm(k_ref[...], pattern)

    ww_keep, ww_send, panel_weights = run(
        "win_weights",
        win_weights,
        [
            shape_of((rows, win_local), bf16),
            shape_of((rows, win_local), bf16),
            shape_of((rows, panel), f32),
        ],
        keep_win,
        *win_pieces,
        scratch=[pltpu.VMEM((rows, win_local), bf16)],
    )
    ww_other = partner(ww_send, "mp", 1)
    gain_own = gain[0].reshape(win_local, stride)[:, 0]
    gain_win = jnp.concatenate([gain_own, partner(gain_own, "mp", 1)])[None]
    factor_other = partner(factor[0], "mp", 1)

    def products(g_ref, k_ref, *refs):
        w_refs, refs = refs[:n_tok], refs[n_tok:]
        own_ref, refs = refs[0], refs[1:]
        count = (n_tok - 1) * n_sec
        x_refs, (keep_ref, send_ref, x_ref, wg) = refs[:count], refs[count:]
        s, t, m = (lax.axis_index(a) for a in ("section", "tok", "mp"))
        fixed = jnp.where(iota2((1, quarter), 1) % stride != 0, g_ref[:, aligned(t, quarter)], 0.0)
        for d in range(n_tok):
            scaled = (w_refs[d][...].astype(f32) * fixed).astype(bf16)
            wg[0, aligned(t ^ d, rows_local), :] = scaled
            kept = scaled * k_ref[aligned(t ^ d, rows_local), :]
            wg[1, aligned((t ^ d ^ (n_tok // 2)), rows_local), :] = kept
        x_ref[:, :tokens, :] = own_ref[...]
        for d in range(1, n_tok):
            for e in range(n_sec):
                x_ref[:, d * tokens : (d + 1) * tokens, aligned(s ^ e, sub)] = x_refs[(d - 1) * n_sec + e][...]
        keep_ref[...] = mm(x_ref[m], wg[m], ((1,), (1,)))
        send_ref[...] = mm(x_ref[1 - m], wg[1 - m], ((1,), (1,))).astype(bf16)

    p_keep, p_send, x_all = run(
        "products",
        products,
        [
            shape_of((token_total, rows), f32),
            shape_of((token_total, rows), bf16),
            shape_of((2, token_total, quarter), bf16),
        ],
        gain,
        keep_q,
        *w_pieces,
        x_own,
        *[p for parts in x_parts for p in parts],
        scratch=[pltpu.VMEM((2, rows, quarter), bf16)],
    )
    p_other = partner(p_send, "mp", 1)

    def products_out(a_ref, b_ref, own_ref, *outs):
        for d in range(n_tok):
            span = slice(d * tokens, (d + 1) * tokens)
            value = a_ref[span, :] + b_ref[span, :].astype(f32)
            if d == 0:
                own_ref[...] = value
            else:
                outs[d - 1][...] = value.astype(bf16)

    p_own, *p_out = run(
        "products_out",
        products_out,
        [shape_of((tokens, rows), f32)] + [shape_of((tokens, rows), bf16)] * (n_tok - 1),
        p_keep,
        p_other,
    )
    p_in = [partner(p, "tok", d + 1) for d, p in enumerate(p_out)]

    def step_of(now, square, fixed_part, gain_now, first_ref, second_ref):
        wide_now = now.astype(f32)
        total = square + jnp.sum(wide_now * wide_now, axis=1, keepdims=True)
        scale = lax.rsqrt(total / width + 1e-06)
        normed_now = (wide_now * scale * gain_now).astype(bf16)
        out = mm(normed_now[:, :win_local], first_ref[...], ((1,), (1,)))
        out = out + mm(normed_now[:, win_local:], second_ref[...], ((1,), (1,)))
        after = (wide_now + (fixed_part * scale + out) * inv_root).astype(bf16)
        return after, normed_now, scale

    carried = shape_of((tokens, rows), bf16)
    square_shape = shape_of((tokens, lanes), f32)

    def first_layer(ba, bb, sa, sb, g_ref, wa, wb, pa, *refs):
        ins, (fixed_ref, now_ref, sq_ref, after_ref) = refs[: n_tok - 1], refs[n_tok - 1 :]
        fixed = pa[...]
        for r in ins:
            fixed = fixed + r[...].astype(f32)
        fixed_ref[...] = fixed
        now_ref[:, :win_local] = ba[...]
        now_ref[:, win_local:] = bb[...]
        sq_ref[...] = sa[...] + sb[...]
        after_ref[...] = step_of(now_ref[...], sq_ref[:, :1], fixed, g_ref[...], wa, wb)[0]

    fixed_part, now, square, after = run(
        "layer_0",
        first_layer,
        [shape_of((tokens, rows), f32), carried, square_shape, carried],
        bw_keep,
        bw_other,
        sq_keep,
        sq_other,
        gain_win,
        ww_keep,
        ww_other,
        p_own,
        *p_in,
    )
    for step in range(1, n_sec):
        arrived = lax.ppermute(after, "section", [(step - 1, step)])
        last = step == n_sec - 1

        def next_layer(now_in, in_ref, sq_ref, g_ref, wa, wb, p_ref, *outs, step=step, last=last):
            here = lax.axis_index("section") == step
            now_value = jnp.where(here, in_ref[...], now_in[...])
            after_value, normed, scale = step_of(
                now_value, sq_ref[:, :1], p_ref[...], g_ref[...], wa, wb
            )
            if not last:
                outs[0][...] = now_value
                outs[1][...] = after_value
                return
            keep_ref, send_ref, normed_keep, normed_send, scale_ref = outs
            keep_ref[...] = after_value[:, :win_local]
            send_ref[...] = after_value[:, win_local:]
            normed_keep[:, :win_local] = normed[:, :win_local]
            normed_send[:, :win_local] = normed[:, win_local:]
            pattern = one_hot((rows, panel), lambda c: (c * panel_step + rows // 2) % rows)
            cols = mm(normed, pattern).astype(bf16)
            normed_keep[:, win_local:] = cols
            normed_send[:, win_local:] = cols
            eye = iota2((tokens, tokens), 0) == iota2((tokens, tokens), 1)
            row = jnp.sum(jnp.where(eye, scale, 0.0), axis=0, keepdims=True)
            scale_ref[...] = jnp.broadcast_to(row, scale_ref.shape)

        if not last:
            outs = [carried, carried]
        else:
            half = shape_of((tokens, win_local), bf16)
            wider = shape_of((tokens, win_local + panel), bf16)
            outs = [half, half, wider, wider, shape_of((8, tokens), f32)]
        result = run(
            f"layer_{step}", next_layer, outs, now, arrived, square, gain_win, ww_keep, ww_other, fixed_part
        )
        if not last:
            now, after = result
    after_keep, after_send, normed_keep, normed_send, scale_own = result
    normed_other = partner(normed_send, "mp", 1)
    scale_other = partner(scale_own, "mp", 1)
    after_other = partner(after_send, "mp", 1)

    def to_tok(a_ref, b_ref, sa, sb, rows_ref, *outs):
        t, m = lax.axis_index("tok"), lax.axis_index("mp")
        first = m == 0
        dense = jnp.where(first, a_ref[:, :win_local], b_ref[:, :win_local])
        pruned = jnp.where(first, b_ref[:, :win_local], a_ref[:, :win_local])
        cols = jnp.where(first, b_ref[:, win_local:], a_ref[:, win_local:])
        rows_ref[...] = jnp.where(
            iota2(rows_ref.shape, 0) == 0,
            jnp.where(first, sa[...], sb[...]),
            jnp.where(first, sb[...], sa[...]),
        )
        shape = (win_local, 2 * win_quarter)
        for d in range(n_tok):
            base = (t ^ d) * win_quarter
            column = iota2(shape, 1)
            row = iota2(shape, 0)
            left = jnp.where((row == column + base) & (column < win_quarter), 1.0, 0.0).astype(bf16)
            right = jnp.where(
                (row == column - win_quarter + base) & (column >= win_quarter), 1.0, 0.0
            ).astype(bf16)
            outs[d][:, :panel] = cols
            outs[d][:, panel:] = (mm(dense, left) + mm(pruned, right)).astype(bf16)

    scale_rows, *buffers = run(
        "to_tok",
        to_tok,
        [shape_of((8, tokens), f32)] + [shape_of((tokens, panel + 2 * win_quarter), bf16)] * n_tok,
        normed_keep,
        normed_other,
        scale_own,
        scale_other,
    )
    buffers = [buffers[0]] + [partner(b, "tok", d + 1) for d, b in enumerate(buffers[1:])]
    scales = gather(scale_rows, "tok")

    def grams(x_ref, g_ref, *refs):
        bufs, refs = refs[:n_tok], refs[n_tok:]
        rows_refs, refs = refs[:n_tok], refs[n_tok:]
        (total_ref, own_ref), outs, scratch = refs[:2], refs[2 : n_tok + 1], refs[n_tok + 1 :]
        t = lax.axis_index("tok")
        (high,) = scratch
        gain_q = g_ref[:, aligned(t, quarter)]
        updated = iota2((1, quarter), 1) % stride == 0
        eye = iota2((tokens, tokens), 0) == iota2((tokens, tokens), 1)
        shape = (2 * win_quarter, quarter)
        for stream in range(2):
            place = jnp.where(
                iota2(shape, 0) * stride - stream * quarter == iota2(shape, 1), 1.0, 0.0
            ).astype(bf16)
            total = None
            for d in range(n_tok):
                scale = jnp.sum(
                    jnp.where(eye, rows_refs[d][stream : stream + 1, :], 0.0), axis=1, keepdims=True
                )
                value = x_ref[stream, d * tokens : (d + 1) * tokens, :].astype(f32) * scale * gain_q
                filled = mm(bufs[d][:, panel:], place)
                normed = jnp.where(updated, filled, value).astype(bf16)
                part = mm(bufs[d][:, :panel], normed, ((0,), (0,)))
                total = part if total is None else total + part
            total = total / token_total
            total_ref[stream] = total
            high[1 - stream] = total.astype(bf16)
        own_ref[...] = high[:, aligned(t, panel_own), :]
        for d in range(1, n_tok):
            outs[d - 1][...] = high[:, aligned(t ^ d, panel_own), :]

    gram_piece = shape_of((2, panel_own, quarter), bf16)
    totals, *gram_pieces = run(
        "grams",
        grams,
        [shape_of((2, panel, quarter), f32)] + [gram_piece] * n_tok,
        x_all,
        gain,
        *buffers,
        *scales,
        scratch=[pltpu.VMEM((2, panel, quarter), bf16)],
    )
    gram_pieces = [gram_pieces[0]] + [partner(p, "tok", d + 1) for d, p in enumerate(gram_pieces[1:])]

    def correct(t_ref, k_ref, fa, fb, *refs):
        w_refs, (keep_ref, send_ref) = refs[:n_tok], refs[n_tok:]
        t, m = lax.axis_index("tok"), lax.axis_index("mp")
        first = m == 0
        upper = jnp.where(first, fa[...], fb[...])
        lower = jnp.where(first, fb[...], fa[...])
        squared = mm(upper, upper, ((0,), (0,)), precision=highest) + mm(
            lower, lower, ((0,), (0,)), precision=highest
        )
        high = [t_ref[i].astype(bf16) for i in range(2)]
        low = [(t_ref[i] - high[i].astype(f32)).astype(bf16) for i in range(2)]
        turn = ((1,), (1,))
        for d in range(n_tok):
            w = w_refs[d][...]
            kept = w * k_ref[aligned(t ^ d, rows_local), :]
            residual = (mm(w, high[0], turn) - mm(kept, high[1], turn)) + (
                mm(w, low[0], turn) - mm(kept, low[1], turn)
            )
            value = mm(residual, squared, precision=highest)
            left, right = value[:, :panel_local], value[:, panel_local:]
            keep_ref[aligned(t ^ d, rows_local), :] = jnp.where(first, left, right)
            send_ref[aligned(t ^ d, rows_local), :] = jnp.where(first, right, left)

    c_keep, c_send = run(
        "correct",
        correct,
        [shape_of((rows, panel_local), f32)] * 2,
        totals,
        keep_q,
        factor[0],
        factor_other,
        *w_pieces,
    )
    c_other = partner(c_send, "mp", 1)

    def pack(a_ref, b_ref, out_ref):
        value = a_ref[...] + b_ref[...]
        out_ref[:, :panel_local] = value[: rows // 2].astype(bf16)
        out_ref[:, panel_local:] = value[rows // 2 :].astype(bf16)

    packed = run("pack", pack, [shape_of((rows // 2, panel), bf16)], c_keep, c_other)[0]
    packs = gather(packed, "tok")

    def finish(*refs):
        gram_refs, refs = refs[:n_tok], refs[n_tok:]
        after_a, after_b, refs = refs[0], refs[1], refs[2:]
        gram_ref, cross_ref, dense_ref, pruned_ref = refs
        t, m = lax.axis_index("tok"), lax.axis_index("mp")
        for d in range(n_tok):
            gram_ref[0, :, aligned(t ^ d, quarter)] = gram_refs[d][0].astype(f32)
            cross_ref[0, :, aligned(t ^ d, quarter)] = gram_refs[d][1].astype(f32)
        first = m == 0
        a, b = after_a[...], after_b[...]
        dense = jnp.where(first, a, b)
        pruned = jnp.where(first, b, a)
        for i in range(micro):
            span = slice(i * tok_rows, (i + 1) * tok_rows)
            dense_ref[0, i] = dense[span]
            pruned_ref[0, i] = pruned[span]

    window_shape = shape_of((1, micro, tok_rows, win_local), bf16)
    gram_shape = shape_of((1, panel_own, width_local), f32)
    gram_out, cross_out, dense_window, pruned_window = run(
        "finish",
        finish,
        [gram_shape, gram_shape, window_shape, window_shape],
        *gram_pieces,
        after_keep,
        after_other,
    )

    def finish_correction(w_ref, *refs):
        ins, (out_ref,) = refs[:n_tok], refs[n_tok:]
        total = tree_sum([r[...].astype(f32) for r in ins])
        value = jnp.concatenate([total[:, :panel_local], total[:, panel_local:]], axis=0)
        out_ref[0] = jnp.where(
            w_ref[:, panel_local:] > 0.5, w_ref[:, :panel_local] + value, 0.0
        )

    corrected = run(
        "finish_correction",
        finish_correction,
        [shape_of((1, rows, panel_local), f32)],
        panel_weights,
        *packs,
    )[0]
    return dense_window, pruned_window, gram_out, cross_out, corrected


def solution(mesh):
    in_specs = (
        P(None, "tok", "mp"),
        P(None, "tok", "mp"),
        P("section", "mp"),
        P("section", "tok", "mp"),
        P("section", None, "mp"),
        P("section", "mp", None),
    )
    out_specs = (
        P("section", None, "tok", "mp"),
        P("section", None, "tok", "mp"),
        P("section", "tok", "mp"),
        P("section", "tok", "mp"),
        P("section", None, "mp"),
    )

    def step(dense_in, pruned_gap, gain, weights, mask_code, factor):
        slice_width = dense_in.shape[2] // (lax.axis_size("tok") * lax.axis_size("section"))
        fits = lax.axis_size("mp") == STREAMS and slice_width % 128 == 0
        form = fast_on_device if fits else on_device
        return form(dense_in, pruned_gap, gain, weights, mask_code, factor)

    return jax.shard_map(
        step, mesh=mesh, in_specs=in_specs, out_specs=out_specs, check_vma=False
    )
```
